32 devices in a mesh: rows: 4 (over x, core), cols: 8 (over z, y).
Axes of the slice: x: 2, y: 2, z: 4, core: 2. Of those that a mesh axis runs over, the one named last changes fastest.
Arguments:
- tensor: float32 [48, 256, 512], P('rows', 'cols'), may hold values from 0 to 1
- first_factor: float32 [48, 256], P('rows', 'cols'), may hold values from -2.5 to 2.5
- second_factor: float32 [256, 256], P('cols', 'rows'), may hold values from -2.5 to 2.5
- third_factor: float32 [512, 256], P(('rows', 'cols')), may hold values from -2.5 to 2.5
Outputs:
- first_new: float32 [48, 256], P('rows', 'cols')
- second_new: float32 [256, 256], P('cols', 'rows')
- third_new: float32 [512, 256], P(('rows', 'cols'))
The draws below stay inside these ranges and needn't reach their ends.
All inputs are finite; a program needn't handle non-finite values.
Results may differ from the reference program's by a relative error of at most 0.0003.
Values sent between devices are 32-bit elements; how exact they have to be, the bound alone decides.
A program may use at most 64 MiB of HBM per device.

```python
import jax
import jax.numpy as jnp
from jax import lax

RANK = 256
K = 512
I_DEV = 12
J_DEV = 32
STEPS = 2
I = 48
J = 256
N_ROWS = 4
N_COLS = 8


def shard_levels(own_key, shape, shards, least, high):
    def one(position, parts):
        draws = jax.random.uniform(jax.random.fold_in(jax.random.fold_in(own_key, 6), position), (parts,), jnp.float32, least / len(shards), high / len(shards))
        return jnp.repeat(jnp.exp(draws), shape[position] // parts).reshape((-1,) + (1,) * (len(shape) - position - 1))

    level = one(*shards[0])
    for cut in shards[1:]:
        level = level * one(*cut)
    return level


def noise(key, extent, deviation, limit, shards=(), kind=jnp.bfloat16):
    values = deviation * jax.random.normal(key, extent, jnp.float32)
    if shards:
        values = values * shard_levels(key, extent, shards, -0.22, 0.18)
    return jnp.clip(values, -limit, limit).astype(kind)


def setup_inputs(seed: int = 0) -> dict:
    splits = jax.random.split(jax.random.key(seed), 5)
    return {
        "tensor": jnp.clip(1.0 * jax.random.uniform(splits[0], (I, J, K), jnp.float32) ** shard_levels(splits[0], (I, J, K), ((0, 4), (1, 8)), -0.2, 0.2), 0.0, 1.0),
        "first_factor": noise(splits[1], (I, RANK), 0.4, 2.5, ((0, 4), (1, 8)), jnp.float32),
        "second_factor": noise(splits[2], (J, RANK), 0.4, 2.5, ((0, 8), (1, 4)), jnp.float32),
        "third_factor": noise(splits[3], (K, RANK), 0.4, 2.5, ((0, 32),), jnp.float32),
    }


def reference(tensor, first_factor, second_factor, third_factor):
    high = lax.Precision.HIGHEST
    size_i = I_DEV * N_ROWS
    size_j = J_DEV * N_COLS
    blocks = tensor.reshape(N_ROWS, I_DEV, size_j, K)
    factor_a, factor_b, factor_c = (first_factor, second_factor, third_factor)
    for step_index in range(STEPS):

        def one_block(carry, inputs):
            grad_b, grad_c = carry
            tile, rows_a = inputs
            khatri = (rows_a[:, None, :] * factor_b[None, :, :]).reshape(-1, RANK)
            model_tile = jnp.dot(khatri, factor_c.T, precision=high, preferred_element_type=jnp.float32)
            deriv = jax.nn.sigmoid(model_tile) - tile.reshape(-1, K)
            deriv_c = jnp.dot(deriv, factor_c, precision=high, preferred_element_type=jnp.float32).reshape(I_DEV, size_j, RANK)
            grad_a = jnp.einsum('ijr,jr->ir', deriv_c, factor_b, precision=high)
            grad_b = grad_b + jnp.einsum('ijr,ir->jr', deriv_c, rows_a, precision=high)
            grad_c = grad_c + lax.dot_general(deriv, khatri, (((0,), (0,)), ((), ())), precision=high, preferred_element_type=jnp.float32)
            return ((grad_b, grad_c), grad_a)
        start = (jnp.zeros((size_j, RANK), jnp.float32), jnp.zeros((K, RANK), jnp.float32))
        (grad_b, grad_c), grad_a = lax.scan(one_block, start, (blocks, factor_a.reshape(N_ROWS, I_DEV, RANK)))
        grad_a = grad_a.reshape(size_i, RANK)
        factor_a = factor_a - 4.0 / jnp.sqrt(jnp.float32(size_j * K)) * grad_a
        factor_b = factor_b - 4.0 / jnp.sqrt(jnp.float32(size_i * K)) * grad_b
        factor_c = factor_c - 4.0 / jnp.sqrt(jnp.float32(size_i * size_j)) * grad_c
    return (factor_a, factor_b, factor_c)
```

```python
import functools

import jax
import jax.numpy as jnp
from jax import lax
from jax.experimental import pallas as pl
from jax.experimental.pallas import tpu as pltpu
from jax.sharding import PartitionSpec as P

STEPS = 2
VMEM_LIMIT = 67043328
MESH = pl.DeviceIdType.MESH


def gather_third(piece):
    return lax.all_gather(piece, ("rows", "cols"), axis=0, tiled=True)


def plain_steps(tensor, first_factor, second_factor, third_factor):
    high = lax.Precision.HIGHEST
    rows_dev, cols_dev, depth = tensor.shape
    rate_a, rate_b, rate_c = rates(tensor)
    flat_target = tensor.reshape(-1, depth)
    shard_a, shard_b = (first_factor, second_factor)
    whole_c = gather_third(third_factor)
    for step_index in range(STEPS):
        whole_a = lax.all_gather(shard_a, "cols", axis=1, tiled=True)
        whole_b = lax.all_gather(shard_b, "rows", axis=1, tiled=True)
        khatri = (whole_a[:, None, :] * whole_b[None, :, :]).reshape(-1, whole_a.shape[1])
        model_tile = jnp.dot(khatri, whole_c.T, precision=high, preferred_element_type=jnp.float32)
        deriv = jax.nn.sigmoid(model_tile) - flat_target
        deriv_c = jnp.dot(
            deriv, whole_c, precision=high, preferred_element_type=jnp.float32
        ).reshape(rows_dev, cols_dev, -1)
        term_a = jnp.einsum("ijr,jr->ir", deriv_c, whole_b, precision=high)
        term_b = jnp.einsum("ijr,ir->jr", deriv_c, whole_a, precision=high)
        term_c = lax.dot_general(
            deriv, khatri, (((0,), (0,)), ((), ())), precision=high,
            preferred_element_type=jnp.float32,
        )
        shard_a = shard_a - rate_a * lax.psum_scatter(
            term_a, "cols", scatter_dimension=1, tiled=True
        )
        shard_b = shard_b - rate_b * lax.psum_scatter(
            term_b, "rows", scatter_dimension=1, tiled=True
        )
        whole_c = whole_c - rate_c * lax.psum(term_c, ("rows", "cols"))
    owner = lax.axis_index("rows") * lax.axis_size("cols") + lax.axis_index("cols")
    count = third_factor.shape[0]
    shard_c = lax.dynamic_slice_in_dim(whole_c, owner * count, count, 0)
    return (shard_a, shard_b, shard_c)


def rates(tensor):
    rows_dev, cols_dev, depth = tensor.shape
    size_i = rows_dev * lax.axis_size("rows")
    size_j = cols_dev * lax.axis_size("cols")
    return (
        4.0 / float(size_j * depth) ** 0.5,
        4.0 / float(size_i * depth) ** 0.5,
        4.0 / float(size_i * size_j) ** 0.5,
    )


def split(x):
    hi = x.astype(jnp.bfloat16)
    return hi, (x - hi.astype(jnp.float32)).astype(jnp.bfloat16)


def dot(lhs, rhs, dims):
    return lax.dot_general(lhs, rhs, (dims, ((), ())), preferred_element_type=jnp.float32)


def kernel(
    n_rows, n_cols, rate, target_hbm, a_hbm, b_hbm, c_hbm, a_out, b_out, c_out,
    stage, target, a_in, b_in, a_parts, b_parts, a_slots, a_rows, a_leave, a_arrive, b_slots,
    c_whole, c_leave, c_arrive, khatri_hi, khatri_lo, deriv, place_a, place_b,
    own_sem, ok_sem, send_sem, recv_sem,
):
    half = n_rows // 2
    n_i, n_j = a_in.shape[0], b_in.shape[0]
    width_a, width_b = a_in.shape[1], b_in.shape[1]
    rank = c_hbm.shape[1]
    depth = target.shape[2]
    row, col = lax.axis_index("rows"), lax.axis_index("cols")
    plane, core = lax.div(row, 2), lax.rem(row, 2)
    used, loads = [], []

    def turn(base, offset, size):
        return lax.rem(base + offset, size)

    def load(src, dst):
        copy = pltpu.make_async_copy(src, dst, own_sem.at[len(loads)])
        loads.append(copy)
        copy.start()
        return copy

    def send(src, dst, to_row, to_col):
        number = len(used)
        copy = pltpu.make_async_remote_copy(
            src_ref=src, dst_ref=dst, send_sem=send_sem.at[number], recv_sem=recv_sem.at[number],
            device_id=(to_row, to_col), device_id_type=MESH,
        )
        used.append(copy)
        copy.start()
        return copy

    steps_away = [(h, flip) for h in range(half) for flip in (0, 1)][1:]
    to_rows = [turn(plane, h, half) * 2 + lax.rem(core + flip, 2) for h, flip in steps_away]
    of_rows = [turn(plane, half - h, half) * 2 + lax.rem(core + flip, 2) for h, flip in steps_away]
    to_cols = [turn(col, k, n_cols) for k in range(1, n_cols)]

    def lanes(block):
        return pl.ds(pl.multiple_of(block * depth, 128), depth)

    def greet(there_row, there_col):
        pl.semaphore_signal(
            barrier, inc=1, device_id=(there_row, there_col), device_id_type=MESH
        )

    barrier = pltpu.get_barrier_semaphore()
    for h in range(1, half):
        greet(turn(plane, h, half) * 2, col)

    @pl.when(core == 1)
    def _():
        greet(row - 1, col)

    for there in to_cols:
        greet(plane * 2 + 1, there)

    got_b = load(b_hbm, b_in)
    got_target = load(target_hbm, stage)
    got_a = load(a_hbm, a_in)
    got_c = load(c_hbm, c_whole.at[0, col])
    got_own = load(target_hbm.at[:, lanes(row)], target.at[row])

    def over_cols(src, dst):
        return [send(src, dst, row, there) for there in to_cols]

    def over_rows(src, dst):
        return [send(src, dst, there, col) for there in to_rows]

    def arrived(copies):
        for copy in copies:
            copy.wait_recv()

    def total(slots, version):
        result = slots[version, 0]
        for k in range(1, slots.shape[1]):
            result = result + slots[version, k]
        return result

    def share(slots, version, place, spread):
        return spread(slots.at[version, place], slots.at[version, place])

    def widen(parts, width):
        per = 128 // width
        pieces = []
        for first in range(0, parts.shape[0], per):
            piece = parts[first]
            for k in range(1, per):
                piece = piece + parts[first + k]
            pieces.append(piece)
        return jnp.concatenate(pieces, axis=1)

    got_b.wait()
    place_b[...] = jnp.zeros_like(place_b)
    place_b[:, :width_b] = b_in[...]
    b_parts[row] = pltpu.roll(place_b[...], lax.rem(row, 128 // width_b) * width_b, 1)
    got_a.wait()
    place_a[...] = jnp.zeros_like(place_a)
    place_a[:n_i, :width_a] = a_in[...]
    a_parts[col] = pltpu.roll(place_a[...], lax.rem(col, 128 // width_a) * width_a, 1)
    got_target.wait()

    @pl.when(core == 0)
    def _():
        pl.semaphore_wait(barrier, n_rows - 1)
        pl.semaphore_signal(ok_sem, inc=1, device_id=(row + 1, col), device_id_type=MESH)

    @pl.when(core == 1)
    def _():
        pl.semaphore_wait(ok_sem, 1)

    sent_b = over_rows(b_parts.at[row], b_parts.at[row])
    sent_target = [send(stage.at[:, lanes(there)], target.at[row], there, col) for there in to_rows]
    got_c.wait()

    @pl.when(core == 1)
    def _():
        pl.semaphore_wait(barrier, 2 * (n_cols - 1))
        pl.semaphore_signal(ok_sem, inc=1, device_id=(row - 1, col), device_id_type=MESH)

    @pl.when(core == 0)
    def _():
        pl.semaphore_wait(ok_sem, 1)

    sent_a = over_cols(a_parts.at[col], a_parts.at[col])
    sent_c = share(c_whole, 0, col, over_cols)
    c_shard = c_whole[0, col]
    arrived(sent_b)
    b_full = widen(b_parts, width_b)
    arrived(sent_a)
    a_own = widen(a_parts, width_a)
    a_rows[0, row] = a_own
    sent_rows = share(a_rows, 0, row, over_rows)
    blocks = [row] + of_rows

    for step in range(STEPS):
        last = step == STEPS - 1
        term = {"c": None, "b": None, "own": None}
        sent_terms = [None] * (n_rows - 1)

        def add(name, value):
            term[name] = value if term[name] is None else term[name] + value

        def build(number):
            block = blocks[number]
            a_block = a_rows[step, block]
            for i in range(n_i):
                hi, lo = split(a_block[i : i + 1, :] * b_full)
                khatri_hi[block, i * n_j : (i + 1) * n_j, :] = hi
                khatri_lo[block, i * n_j : (i + 1) * n_j, :] = lo

        def probability(number):
            block = blocks[number]
            both = dot(khatri_hi[block], c_tall, ((1,), (1,)))
            model = both[:, :depth] + (both[:, depth:] + dot(khatri_lo[block], c_hi, ((1,), (1,))))
            return jax.nn.sigmoid(model)

        def derive(number, prob):
            block = blocks[number]
            hi, lo = split(prob - target[block])
            deriv[block, :, :depth] = hi
            deriv[block, :, depth:] = lo

        def third(number):
            block = blocks[number]
            both = dot(deriv[block], khatri_hi[block], ((0,), (0,)))
            cross = dot(deriv[block, :, :depth], khatri_lo[block], ((0,), (0,)))
            add("c", both[:depth] + (both[depth:] + cross))

        def others(number):
            block = blocks[number]
            deriv_c = dot(deriv[block], c_twice, ((1,), (0,)))
            deriv_c = deriv_c + dot(deriv[block, :, :depth], c_lo, ((1,), (0,)))
            deriv_c = deriv_c.reshape(n_i, n_j, rank)
            term_a = jnp.sum(deriv_c * b_full[None, :, :], axis=1)
            if number:
                a_leave[step, number - 1] = jnp.zeros_like(a_own)
                a_leave[step, number - 1, :n_i, :] = term_a
            else:
                term["own"] = term_a
            a_block = a_rows[step, block][:n_i, :]
            add("b", jnp.sum(deriv_c * a_block[:, None, :], axis=0))

        def deliver(number):
            sent_terms[number - 1] = send(
                a_leave.at[step, number - 1], a_arrive.at[step, number - 1], blocks[number], col
            )

        near, far = [0, 1], list(range(2, n_rows))
        build(0)
        if step == 0:
            arrived(sent_c)
        else:
            arrived(sent_rows)
            for number in [1] + far:
                build(number)
            arrived(sent_c)
        c_hi, c_lo = split(c_whole[step].reshape(-1, rank))
        c_tall = jnp.concatenate([c_hi, c_lo], axis=0)
        c_twice = jnp.concatenate([c_hi, c_hi], axis=0)
        if step == 0:
            prob = probability(0)
            got_own.wait()
            derive(0, prob)
            third(0)
            others(0)
            sent_rows[0].wait_recv()
            build(1)
            prob = probability(1)
            sent_target[0].wait_recv()
            derive(1, prob)
            third(1)
            others(1)
            deliver(1)
            arrived(sent_rows[1:])
            probs = []
            for number in far:
                build(number)
                probs.append(probability(number))
            arrived(sent_target[1:])
            for number, prob in zip(far, probs):
                derive(number, prob)
            for number in far:
                others(number)
            for number in far:
                deliver(number)
            for number in far:
                third(number)
        else:
            for number in far + near:
                derive(number, probability(number))
            for number in far:
                others(number)
            for number in far:
                deliver(number)
            for number in far + near:
                third(number)
        c_leave[step] = term["c"].reshape(c_leave.shape[1:])
        sent_c = [
            send(c_leave.at[step, there], c_arrive.at[step, k], row, there)
            for k, there in enumerate(to_cols)
        ]
        if step:
            others(1)
            deliver(1)
            others(0)
        b_slots[step, row] = term["b"]
        sent_b = share(b_slots, step, row, over_rows)
        a_leave[step, n_rows - 1] = jnp.zeros_like(a_own)
        a_leave[step, n_rows - 1, :n_i, :] = term["own"]
        arrived(sent_terms)
        term_own = a_leave[step, n_rows - 1]
        for k in range(n_rows - 1):
            term_own = term_own + a_arrive[step, k]
        a_slots[step, col] = term_own
        sent_a = share(a_slots, step, col, over_cols)
        arrived(sent_c)
        grad_c = c_leave[step, col]
        for k in range(n_cols - 1):
            grad_c = grad_c + c_arrive[step, k]
        c_shard = c_shard - rate[2] * grad_c
        if last:
            c_out[...] = c_shard
        else:
            c_whole[step + 1, col] = c_shard
            sent_c = share(c_whole, step + 1, col, over_cols)
        arrived(sent_b)
        b_full = b_full - rate[1] * total(b_slots, step)
        arrived(sent_a)
        a_own = a_own - rate[0] * total(a_slots, step)
        if not last:
            a_rows[step + 1, row] = a_own
            sent_rows = share(a_rows, step + 1, row, over_rows)
    back = lax.rem(n_cols - col, n_cols) * width_a
    a_out[...] = pltpu.roll(a_own, back, 1)[:n_i, :width_a]
    back = lax.rem(n_rows - row, n_rows) * width_b
    b_out[...] = pltpu.roll(b_full, back, 1)[:, :width_b]
    for copy in used:
        copy.wait_send()


def write_kernel(a_ref, b_ref, c_ref, a_out, b_out, c_out, sems):
    copies = [
        pltpu.make_async_copy(src, dst, sems.at[k])
        for k, (src, dst) in enumerate(((a_ref, a_out), (b_ref, b_out), (c_ref, c_out)))
    ]
    for copy in copies:
        copy.start()
    for copy in copies:
        copy.wait()


def n_copies(n_rows, n_cols):
    rows, cols = n_rows - 1, n_cols - 1
    return rows + (STEPS + 1) * (cols + rows) + STEPS * (rows + cols) + STEPS * (rows + cols)


def per_device(tensor, first_factor, second_factor, third_factor):
    n_rows, n_cols = lax.axis_size("rows"), lax.axis_size("cols")
    count, rank = third_factor.shape
    n_i, n_j, depth = tensor.shape
    part = depth // n_rows
    width_a, width_b = first_factor.shape[1], second_factor.shape[1]
    uneven = rank % 128 or width_a > 128 or 128 % width_a or width_b > 128 or 128 % width_b
    if count % 8 or n_rows % 2 or n_rows < 4 or n_j % 16 or part != 128 or uneven:
        return plain_steps(tensor, first_factor, second_factor, third_factor)
    tall = -(-n_i // 8) * 8
    f32, bf16 = jnp.float32, jnp.bfloat16
    copies = n_copies(n_rows, n_cols)
    vmem = pl.BlockSpec(memory_space=pltpu.VMEM)
    hbm = pl.BlockSpec(memory_space=pl.ANY)
    shapes = tuple(
        jax.ShapeDtypeStruct(x.shape, f32) for x in (first_factor, second_factor, third_factor)
    )
    results = pl.pallas_call(
        functools.partial(kernel, n_rows, n_cols, rates(tensor)),
        out_shape=shapes,
        in_specs=[hbm] * 4,
        out_specs=(vmem,) * 3,
        scratch_shapes=[
            pltpu.VMEM((n_i * n_j, depth), f32),
            pltpu.VMEM((n_rows, n_i * n_j, part), f32),
            pltpu.VMEM((n_i, width_a), f32),
            pltpu.VMEM((n_j, width_b), f32),
            pltpu.VMEM((n_cols, tall, 128), f32),
            pltpu.VMEM((n_rows, n_j, 128), f32),
            pltpu.VMEM((STEPS, n_cols, tall, rank), f32),
            pltpu.VMEM((STEPS, n_rows, tall, rank), f32),
            pltpu.VMEM((STEPS, n_rows, tall, rank), f32),
            pltpu.VMEM((STEPS, n_rows - 1, tall, rank), f32),
            pltpu.VMEM((STEPS, n_rows, n_j, rank), f32),
            pltpu.VMEM((STEPS, n_cols, count, rank), f32),
            pltpu.VMEM((STEPS, n_cols, count, rank), f32),
            pltpu.VMEM((STEPS, n_cols - 1, count, rank), f32),
            pltpu.VMEM((n_rows, n_i * n_j, rank), bf16),
            pltpu.VMEM((n_rows, n_i * n_j, rank), bf16),
            pltpu.VMEM((n_rows, n_i * n_j, 2 * part), bf16),
            pltpu.VMEM((tall, 128), f32),
            pltpu.VMEM((n_j, 128), f32),
            pltpu.SemaphoreType.DMA((5,)),
            pltpu.SemaphoreType.REGULAR,
            pltpu.SemaphoreType.DMA((copies,)),
            pltpu.SemaphoreType.DMA((copies,)),
        ],
        compiler_params=pltpu.CompilerParams(
            collective_id=0, has_side_effects=True, vmem_limit_bytes=VMEM_LIMIT
        ),
    )(tensor.reshape(n_i * n_j, depth), first_factor, second_factor, third_factor)
    return pl.pallas_call(
        write_kernel,
        out_shape=shapes,
        in_specs=[vmem] * 3,
        out_specs=(hbm,) * 3,
        scratch_shapes=[pltpu.SemaphoreType.DMA((3,))],
    )(*results)


def solution(mesh):
    in_specs = (
        P("rows", "cols", None),
        P("rows", "cols"),
        P("cols", "rows"),
        P(("rows", "cols"), None),
    )
    out_specs = (P("rows", "cols"), P("cols", "rows"), P(("rows", "cols"), None))
    return jax.shard_map(
        per_device, mesh=mesh, in_specs=in_specs, out_specs=out_specs, check_vma=False
    )
```

```python
import functools

import jax
import jax.numpy as jnp
from jax import lax
from jax.experimental import pallas as pl
from jax.experimental.pallas import tpu as pltpu
from jax.sharding import PartitionSpec as P

STEPS = 2
VMEM_LIMIT = 48 << 20
MESH = pl.DeviceIdType.MESH


def gather_third(piece):
    return lax.all_gather(piece, ("rows", "cols"), axis=0, tiled=True)


def plain_steps(tensor, first_factor, second_factor, third_factor):
    high = lax.Precision.HIGHEST
    rows_dev, cols_dev, depth = tensor.shape
    rate_a, rate_b, rate_c = rates(tensor)
    flat_target = tensor.reshape(-1, depth)
    shard_a, shard_b = (first_factor, second_factor)
    whole_c = gather_third(third_factor)
    for step_index in range(STEPS):
        whole_a = lax.all_gather(shard_a, "cols", axis=1, tiled=True)
        whole_b = lax.all_gather(shard_b, "rows", axis=1, tiled=True)
        khatri = (whole_a[:, None, :] * whole_b[None, :, :]).reshape(-1, whole_a.shape[1])
        model_tile = jnp.dot(khatri, whole_c.T, precision=high, preferred_element_type=jnp.float32)
        deriv = jax.nn.sigmoid(model_tile) - flat_target
        deriv_c = jnp.dot(
            deriv, whole_c, precision=high, preferred_element_type=jnp.float32
        ).reshape(rows_dev, cols_dev, -1)
        term_a = jnp.einsum("ijr,jr->ir", deriv_c, whole_b, precision=high)
        term_b = jnp.einsum("ijr,ir->jr", deriv_c, whole_a, precision=high)
        term_c = lax.dot_general(
            deriv, khatri, (((0,), (0,)), ((), ())), precision=high,
            preferred_element_type=jnp.float32,
        )
        shard_a = shard_a - rate_a * lax.psum_scatter(
            term_a, "cols", scatter_dimension=1, tiled=True
        )
        shard_b = shard_b - rate_b * lax.psum_scatter(
            term_b, "rows", scatter_dimension=1, tiled=True
        )
        whole_c = whole_c - rate_c * lax.psum(term_c, ("rows", "cols"))
    owner = lax.axis_index("rows") * lax.axis_size("cols") + lax.axis_index("cols")
    count = third_factor.shape[0]
    shard_c = lax.dynamic_slice_in_dim(whole_c, owner * count, count, 0)
    return (shard_a, shard_b, shard_c)


def rates(tensor):
    rows_dev, cols_dev, depth = tensor.shape
    size_i = rows_dev * lax.axis_size("rows")
    size_j = cols_dev * lax.axis_size("cols")
    return (
        4.0 / float(size_j * depth) ** 0.5,
        4.0 / float(size_i * depth) ** 0.5,
        4.0 / float(size_i * size_j) ** 0.5,
    )


def split(x):
    hi = x.astype(jnp.bfloat16)
    return hi, (x - hi.astype(jnp.float32)).astype(jnp.bfloat16)


def dot(lhs, rhs, dims):
    return lax.dot_general(lhs, rhs, (dims, ((), ())), preferred_element_type=jnp.float32)


def kernel(
    n_rows, n_cols, rate, target_hbm, a_hbm, b_hbm, c_hbm, a_out, b_out, c_out,
    stage, target, a_in, b_in, a_parts, b_parts, a_slots, a_rows, a_leave, a_arrive, b_slots,
    c_whole, c_leave, c_arrive, khatri_hi, khatri_lo, deriv, place_a, place_b,
    own_sem, ok_sem, send_sem, recv_sem,
):
    half = n_rows // 2
    n_i, n_j = a_in.shape[0], b_in.shape[0]
    width_a, width_b = a_in.shape[1], b_in.shape[1]
    rank = c_hbm.shape[1]
    depth = target.shape[2]
    row, col = lax.axis_index("rows"), lax.axis_index("cols")
    plane, core = lax.div(row, 2), lax.rem(row, 2)
    used, loads, gone = [], [], set()

    def turn(base, offset, size):
        return lax.rem(base + offset, size)

    def load(src, dst):
        copy = pltpu.make_async_copy(src, dst, own_sem.at[len(loads)])
        loads.append(copy)
        copy.start()
        return copy

    def send(src, dst, to_row, to_col):
        number = len(used)
        copy = pltpu.make_async_remote_copy(
            src_ref=src, dst_ref=dst, send_sem=send_sem.at[number], recv_sem=recv_sem.at[number],
            device_id=(to_row, to_col), device_id_type=MESH,
        )
        used.append(copy)
        copy.start()
        return copy

    def flipped(place, mask):
        for bit in (1 << k for k in range(mask.bit_length()) if mask >> k & 1):
            place = place + bit - 2 * bit * lax.rem(lax.div(place, bit), 2)
        return place

    steps_away = [(h, flip) for h in range(half) for flip in (0, 1)][1:]
    to_rows = [turn(plane, h, half) * 2 + lax.rem(core + flip, 2) for h, flip in steps_away]
    of_rows = [turn(plane, half - h, half) * 2 + lax.rem(core + flip, 2) for h, flip in steps_away]
    to_cols = [flipped(col, mask) for mask in reversed(range(1, n_cols))]

    def lanes(block):
        return pl.ds(pl.multiple_of(block * depth, 128), depth)

    def tile(there):
        return pl.ds(pl.multiple_of(lax.div(there * width_a, 128) * 128, 128), 128)

    def greet(there_row, there_col):
        pl.semaphore_signal(
            barrier, inc=1, device_id=(there_row, there_col), device_id_type=MESH
        )

    barrier = pltpu.get_barrier_semaphore()
    for h in range(1, half):
        greet(turn(plane, h, half) * 2, col)

    @pl.when(core == 1)
    def _():
        greet(row - 1, col)

    for there in to_cols:
        greet(plane * 2 + 1, there)

    got_b = load(b_hbm, b_in)
    got_target = [
        load(target_hbm.at[:, lanes(there)], stage.at[k]) for k, there in enumerate(to_rows)
    ]
    got_a = load(a_hbm, a_in)
    got_c = load(c_hbm, c_whole.at[0, col])
    got_own = load(target_hbm.at[:, lanes(row)], target.at[row])

    def left(copies):
        for copy in copies:
            if id(copy) not in gone:
                gone.add(id(copy))
                copy.wait_send()

    def over_cols(src, dst):
        return [send(src, dst, row, there) for there in to_cols]

    def over_rows(src, dst):
        return [send(src, dst, there, col) for there in to_rows]

    def arrived(copies):
        for copy in copies:
            copy.wait_recv()

    def total(slots, version):
        result = slots[version, 0]
        for k in range(1, slots.shape[1]):
            result = result + slots[version, k]
        return result

    def share(slots, version, place, spread):
        return spread(slots.at[version, place], slots.at[version, place])

    def widen(parts, width):
        per = 128 // width
        pieces = []
        for first in range(0, parts.shape[0], per):
            piece = parts[first]
            for k in range(1, per):
                piece = piece + parts[first + k]
            pieces.append(piece)
        return jnp.concatenate(pieces, axis=1)

    got_b.wait()
    place_b[...] = jnp.zeros_like(place_b)
    place_b[:, :width_b] = b_in[...]
    b_parts[row] = pltpu.roll(place_b[...], lax.rem(row, 128 // width_b) * width_b, 1)
    got_a.wait()
    place_a[...] = jnp.zeros_like(place_a)
    place_a[:n_i, :width_a] = a_in[...]
    a_parts[col] = pltpu.roll(place_a[...], lax.rem(col, 128 // width_a) * width_a, 1)
    for copy in got_target:
        copy.wait()

    @pl.when(core == 0)
    def _():
        pl.semaphore_wait(barrier, n_rows - 1)
        pl.semaphore_signal(ok_sem, inc=1, device_id=(row + 1, col), device_id_type=MESH)

    @pl.when(core == 1)
    def _():
        pl.semaphore_wait(ok_sem, 1)

    sent_b = over_rows(b_parts.at[row], b_parts.at[row])
    sent_target = [
        send(stage.at[k], target.at[row], there, col) for k, there in enumerate(to_rows[:-1])
    ]
    rows_dev = n_i * n_j
    early = rows_dev * 3 // 4 // 8 * 8
    sent_target.append(
        send(
            stage.at[n_rows - 2, :early], target.at[row, :early], to_rows[-1], col
        )
    )
    got_c.wait()

    @pl.when(core == 1)
    def _():
        pl.semaphore_wait(barrier, 2 * (n_cols - 1))
        pl.semaphore_signal(ok_sem, inc=1, device_id=(row - 1, col), device_id_type=MESH)

    @pl.when(core == 0)
    def _():
        pl.semaphore_wait(ok_sem, 1)

    sent_a = over_cols(a_parts.at[col], a_parts.at[col])
    sent_c = share(c_whole, 0, col, over_cols)
    c_shard = c_whole[0, col]
    arrived(sent_b)
    b_full = widen(b_parts, width_b)
    arrived(sent_a)
    a_own = widen(a_parts, width_a)
    a_rows[0, row] = a_own
    sent_rows = share(a_rows, 0, row, over_rows)
    sent_target.append(
        send(
            stage.at[n_rows - 2, early:], target.at[row, early:], to_rows[-1], col
        )
    )
    blocks = [row] + of_rows

    for step in range(STEPS):
        last = step == STEPS - 1
        term = {"c": None, "b": None, "own": None}
        sent_terms = [None] * (n_rows - 1)

        def add(name, value):
            term[name] = value if term[name] is None else term[name] + value

        def build(number):
            block = blocks[number]
            a_block = a_rows[step, block]
            for i in range(n_i):
                hi, lo = split(a_block[i : i + 1, :] * b_full)
                khatri_hi[block, i * n_j : (i + 1) * n_j, :] = hi
                khatri_lo[block, i * n_j : (i + 1) * n_j, :] = lo

        def probability(number):
            block = blocks[number]
            both = dot(khatri_hi[block], c_tall, ((1,), (1,)))
            model = both[:, :depth] + (both[:, depth:] + dot(khatri_lo[block], c_hi, ((1,), (1,))))
            return jax.nn.sigmoid(model)

        def derive(number, prob):
            block = blocks[number]
            hi, lo = split(prob - target[block])
            deriv[block, :, :depth] = hi
            deriv[block, :, depth:] = lo

        def third(number):
            block = blocks[number]
            both = dot(deriv[block], khatri_hi[block], ((0,), (0,)))
            cross = dot(deriv[block, :, :depth], khatri_lo[block], ((0,), (0,)))
            add("c", both[:depth] + (both[depth:] + cross))

        def others(number):
            block = blocks[number]
            deriv_c = dot(deriv[block], c_twice, ((1,), (0,)))
            deriv_c = deriv_c + dot(deriv[block, :, :depth], c_lo, ((1,), (0,)))
            deriv_c = deriv_c.reshape(n_i, n_j, rank)
            term_a = jnp.sum(deriv_c * b_full[None, :, :], axis=1)
            if number:
                a_leave[step, number - 1] = jnp.zeros_like(a_own)
                a_leave[step, number - 1, :n_i, :] = term_a
            else:
                term["own"] = term_a
            a_block = a_rows[step, block][:n_i, :]
            add("b", jnp.sum(deriv_c * a_block[:, None, :], axis=0))

        def deliver(number):
            sent_terms[number - 1] = send(
                a_leave.at[step, number - 1], a_arrive.at[step, number - 1], blocks[number], col
            )

        near, far = [0, 1], list(range(2, n_rows))
        build(0)
        if step == 0:
            arrived(sent_c)
        else:
            arrived(sent_rows)
            for number in [1] + far:
                build(number)
            arrived(sent_c)
        c_hi, c_lo = split(c_whole[step].reshape(-1, rank))
        c_tall = jnp.concatenate([c_hi, c_lo], axis=0)
        c_twice = jnp.concatenate([c_hi, c_hi], axis=0)
        if step == 0:
            prob = probability(0)
            got_own.wait()
            derive(0, prob)
            third(0)
            others(0)
            sent_rows[0].wait_recv()
            build(1)
            prob = probability(1)
            sent_target[0].wait_recv()
            derive(1, prob)
            third(1)
            others(1)
            deliver(1)
            arrived(sent_rows[1:])
            probs = []
            for number in far:
                build(number)
                probs.append(probability(number))
            arrived(sent_target[1:])
            for number, prob in zip(far, probs):
                derive(number, prob)
            for number in far:
                others(number)
            for number in far:
                deliver(number)
            for number in far:
                third(number)
        else:
            for number in far + near:
                derive(number, probability(number))
            for number in far:
                others(number)
            for number in far:
                deliver(number)
            for number in far + near:
                third(number)
        c_leave[step] = term["c"].reshape(c_leave.shape[1:])
        sent_c = [
            send(c_leave.at[step, there], c_arrive.at[step, k], row, there)
            for k, there in enumerate(to_cols)
        ]
        if step:
            others(1)
            deliver(1)
            others(0)
        b_slots[step, row] = term["b"]
        sent_b = share(b_slots, step, row, over_rows)
        a_leave[step, n_rows - 1] = jnp.zeros_like(a_own)
        a_leave[step, n_rows - 1, :n_i, :] = term["own"]
        arrived(sent_terms)
        term_own = a_leave[step, n_rows - 1]
        for k in range(n_rows - 1):
            term_own = term_own + a_arrive[step, k]
        a_slots[step, col] = term_own
        if last:
            sent_a = [
                send(
                    a_slots.at[step, col, :, tile(there)], a_slots.at[step, col, :, tile(there)],
                    row, there,
                )
                for there in to_cols
            ]
        else:
            sent_a = share(a_slots, step, col, over_cols)
        left(used if last else used[: -n_cols + 1])
        arrived(sent_c)
        grad_c = c_leave[step, col]
        for k in range(n_cols - 1):
            grad_c = grad_c + c_arrive[step, k]
        c_shard = c_shard - rate[2] * grad_c
        if last:
            c_out[...] = c_shard
        else:
            c_whole[step + 1, col] = c_shard
            sent_c = share(c_whole, step + 1, col, over_cols)
        arrived(sent_b)
        b_full = b_full - rate[1] * total(b_slots, step)
        arrived(sent_a)
        if not last:
            a_own = a_own - rate[0] * total(a_slots, step)
            a_rows[step + 1, row] = a_own
            sent_rows = share(a_rows, step + 1, row, over_rows)
    grad_a = a_slots[STEPS - 1, 0, :, tile(col)]
    for k in range(1, n_cols):
        grad_a = grad_a + a_slots[STEPS - 1, k, :, tile(col)]
    a_own = a_rows[STEPS - 1, row, :, tile(col)] - rate[0] * grad_a
    per = 128 // width_a
    back = lax.rem(per - lax.rem(col, per), per) * width_a
    a_out[...] = pltpu.roll(a_own, back, 1)[:n_i, :width_a]
    back = lax.rem(n_rows - row, n_rows) * width_b
    b_out[...] = pltpu.roll(b_full, back, 1)[:, :width_b]
    left(used)


def write_kernel(a_ref, b_ref, c_ref, a_out, b_out, c_out, sems):
    copies = [
        pltpu.make_async_copy(src, dst, sems.at[k])
        for k, (src, dst) in enumerate(((a_ref, a_out), (b_ref, b_out), (c_ref, c_out)))
    ]
    for copy in copies:
        copy.start()
    for copy in copies:
        copy.wait()


def n_copies(n_rows, n_cols):
    rows, cols = n_rows - 1, n_cols - 1
    return 1 + rows + (STEPS + 1) * (cols + rows) + STEPS * (rows + cols) + STEPS * (rows + cols)


def per_device(tensor, first_factor, second_factor, third_factor):
    n_rows, n_cols = lax.axis_size("rows"), lax.axis_size("cols")
    count, rank = third_factor.shape
    n_i, n_j, depth = tensor.shape
    part = depth // n_rows
    width_a, width_b = first_factor.shape[1], second_factor.shape[1]
    uneven = rank % 128 or width_a > 128 or 128 % width_a or width_b > 128 or 128 % width_b
    if count % 8 or n_rows % 2 or n_rows < 4 or n_cols & (n_cols - 1) or n_j % 16 or part != 128 or uneven:
        return plain_steps(tensor, first_factor, second_factor, third_factor)
    tall = -(-n_i // 8) * 8
    f32, bf16 = jnp.float32, jnp.bfloat16
    copies = n_copies(n_rows, n_cols)
    vmem = pl.BlockSpec(memory_space=pltpu.VMEM)
    hbm = pl.BlockSpec(memory_space=pl.ANY)
    shapes = tuple(
        jax.ShapeDtypeStruct(x.shape, f32) for x in (first_factor, second_factor, third_factor)
    )
    results = pl.pallas_call(
        functools.partial(kernel, n_rows, n_cols, rates(tensor)),
        out_shape=shapes,
        in_specs=[hbm] * 4,
        out_specs=(vmem,) * 3,
        scratch_shapes=[
            pltpu.VMEM((n_rows - 1, n_i * n_j, part), f32),
            pltpu.VMEM((n_rows, n_i * n_j, part), f32),
            pltpu.VMEM((n_i, width_a), f32),
            pltpu.VMEM((n_j, width_b), f32),
            pltpu.VMEM((n_cols, tall, 128), f32),
            pltpu.VMEM((n_rows, n_j, 128), f32),
            pltpu.VMEM((STEPS, n_cols, tall, rank), f32),
            pltpu.VMEM((STEPS, n_rows, tall, rank), f32),
            pltpu.VMEM((STEPS, n_rows, tall, rank), f32),
            pltpu.VMEM((STEPS, n_rows - 1, tall, rank), f32),
            pltpu.VMEM((STEPS, n_rows, n_j, rank), f32),
            pltpu.VMEM((STEPS, n_cols, count, rank), f32),
            pltpu.VMEM((STEPS, n_cols, count, rank), f32),
            pltpu.VMEM((STEPS, n_cols - 1, count, rank), f32),
            pltpu.VMEM((n_rows, n_i * n_j, rank), bf16),
            pltpu.VMEM((n_rows, n_i * n_j, rank), bf16),
            pltpu.VMEM((n_rows, n_i * n_j, 2 * part), bf16),
            pltpu.VMEM((tall, 128), f32),
            pltpu.VMEM((n_j, 128), f32),
            pltpu.SemaphoreType.DMA((n_rows + 3,)),
            pltpu.SemaphoreType.REGULAR,
            pltpu.SemaphoreType.DMA((copies,)),
            pltpu.SemaphoreType.DMA((copies,)),
        ],
        compiler_params=pltpu.CompilerParams(
            collective_id=0, has_side_effects=True, vmem_limit_bytes=VMEM_LIMIT
        ),
    )(*[pltpu.with_memory_space_constraint(x, pltpu.HBM) for x in (tensor.reshape(n_i * n_j, depth), first_factor, second_factor, third_factor)])
    return pl.pallas_call(
        write_kernel,
        out_shape=shapes,
        in_specs=[vmem] * 3,
        out_specs=(hbm,) * 3,
        scratch_shapes=[pltpu.SemaphoreType.DMA((3,))],
        compiler_params=pltpu.CompilerParams(vmem_limit_bytes=1 << 20),
    )(*results)


def solution(mesh):
    in_specs = (
        P("rows", "cols", None),
        P("rows", "cols"),
        P("cols", "rows"),
        P(("rows", "cols"), None),
    )
    out_specs = (P("rows", "cols"), P("cols", "rows"), P(("rows", "cols"), None))
    return jax.shard_map(
        per_device, mesh=mesh, in_specs=in_specs, out_specs=out_specs, check_vma=False
    )
```
